256 devices in a mesh: pipe: 8 (over y, core), expert: 32 (over x, z).
Axes of the slice: x: 4, y: 4, z: 8, core: 2. Of those that a mesh axis runs over, the one named last changes fastest.
Arguments:
- saved_inputs: bfloat16 [8, 4096, 2048], P('pipe', 'expert'), may hold values from -6 to 6
- grad_out: bfloat16 [8, 4096, 2048], P('pipe', 'expert'), may hold values from -6 to 6
- routes: int32 [8, 4096, 8], P('pipe', 'expert'), may hold values from 0 to 31, all different within a row; in each aligned block of 128 rows (0 to 127, 128 to 255, ..., all dimensions but the last counted through in order) at most 36 rows name the same one
- route_probs: float32 [8, 4096, 8], P('pipe', 'expert'), may hold values from 0.1 to 0.6
- w_in: bfloat16 [8, 32, 2048, 768], P('pipe', 'expert'), may hold values from -0.125 to 0.125
- w_out: bfloat16 [8, 32, 384, 2048], P('pipe', 'expert'), may hold values from -0.3125 to 0.3125
Outputs:
- grad_tokens: float32 [8, 4096, 2048], P('pipe', 'expert')
- grad_w_in: bfloat16 [8, 32, 2048, 768], P('pipe', 'expert')
- grad_w_out: bfloat16 [8, 32, 384, 2048], P('pipe', 'expert')
The draws below stay inside these ranges and needn't reach their ends.
Inputs may be any that keep to these rules, and one draw needn't show every extreme that they name: `routes`: each row names 8 different experts. Among the rows of one device (aligned blocks of 128 rows) no expert is named more than 36 times, a bound that some block reaches.
All inputs are finite; a program needn't handle non-finite values.
Results may differ from the reference program's by a relative error of at most 0.0057.
Values may be sent and summed in bfloat16 or wider, within the bound.
No kernel may reach another device: no remote copies, remote signals or barrier semaphores. Data moves between devices by JAX's collectives and lax.ppermute only.
A program may use at most 128 MiB of HBM per device.

```python
import math
import jax
import jax.numpy as jnp
import numpy as np
from jax import lax

D = 2048
FF = 384
TOP = 8
EXPERTS = 32
TOK_DEV = 128
CAP = 36
TOKENS = 4096
N_PIPE = 8
N_EXPERT = 32


def shard_levels(key, extent, cuts, low, top_value):
    factor_of = 1.0
    for dim, parts in cuts:
        draws = jax.random.uniform(jax.random.fold_in(jax.random.fold_in(key, 6), dim), (parts,), jnp.float32, low / len(cuts), top_value / len(cuts))
        factor_of = factor_of * jnp.repeat(jnp.exp(draws), extent[dim] // parts).reshape((-1,) + (1,) * (len(extent) - 1 - dim))
    return factor_of


def shared_out(stream_key, own, number, rows, amount, top, most, skew):
    sequence = jax.random.permutation(stream_key, amount)
    crowded, ordinary = load_shares(amount, rows * top, most, skew, True), load_shares(amount, rows * top, most, skew, False)
    places = jnp.arange(amount)

    def named(sizes, rotation):
        used = int((sizes > 0).sum())
        fixed = max(1, used // 4)
        moved = fixed + (places - fixed + rotation * (used - fixed)) % max(1, amount - fixed)
        return jnp.zeros((amount,), jnp.int32).at[sequence[jnp.where(places < fixed, places, moved)]].set(jnp.asarray(sizes, jnp.int32))

    sizes = jnp.where(number % 4 == 0, named(crowded, number // 4), named(ordinary, number - number // 4 - 1))
    mixed = jax.random.permutation(jax.random.fold_in(own, 3), amount)
    donor, taker = mixed[0:amount // 2 * 2:2], mixed[1:amount // 2 * 2:2]
    margin = jnp.minimum(sizes[donor] - 1, most - sizes[taker]) // 2
    margin = jnp.where((donor == sequence[0]) | (taker == sequence[0]) | (sizes[taker] == 0), 0, jnp.maximum(margin, 0))
    moved = jax.random.randint(jax.random.fold_in(own, 4), (amount // 2,), 0, 1 << 20) % (margin + 1)
    sizes = sizes.at[donor].add(-moved).at[taker].add(moved)
    labels = jnp.searchsorted(jnp.cumsum(sizes), jnp.arange(rows * top), side="right").astype(jnp.int32)
    grid = labels.reshape(top, rows).T
    grid = grid[jax.random.permutation(jax.random.fold_in(own, 1), rows)]
    rotation = jax.random.randint(jax.random.fold_in(own, 2), (rows, 1), 0, top)
    return jnp.take_along_axis(grid, (jnp.arange(top)[None, :] + rotation) % top, axis=1)


def load_shares(amount, total, limit, lean, full):
    portions = [(1 << 20) // math.isqrt(standing ** lean) + 1 for standing in range(1, amount + 1)]
    largest = limit if full else min(limit, max(-(-total // amount), total * portions[0] // sum(portions)))
    least = 1 if total - largest >= amount - 1 else 0
    holding, rest = [largest] + [least] * (amount - 1), total - largest - least * (amount - 1)
    while rest > 0:
        candidates = [i for i in range(1, amount) if holding[i] < largest] or [i for i in range(1, amount) if holding[i] < limit]
        mass, left = sum([portions[i] for i in candidates]), rest
        for i in candidates:
            more = min(limit - holding[i], max(1, left * portions[i] // mass), rest)
            holding[i] = holding[i] + more
            rest = rest - more
    return np.array(holding)


def normal_values(rng, shape, spread, bound, shards=(), kind=jnp.bfloat16):
    factor_of = shard_levels(rng, shape, shards, -0.22, 0.18) if shards else 1.0
    entries = jax.random.normal(rng, shape, jnp.float32) * spread * factor_of
    return jnp.minimum(jnp.maximum(entries, -bound), bound).astype(kind)


def setup_inputs(seed: int = 0) -> dict:
    arg_keys = jax.random.split(jax.random.key(seed), 7)
    saved_inputs = normal_values(arg_keys[0], (N_PIPE, TOKENS, D), 1.0, 6.0, ((0, 8), (1, 32)))
    grad_out = normal_values(arg_keys[1], (N_PIPE, TOKENS, D), 1.0, 6.0, ((0, 8), (1, 32)))
    routes_keys = jax.random.split(jax.random.fold_in(arg_keys[2], 1), N_PIPE * TOKENS // TOK_DEV)
    routes_turns = jax.random.permutation(jax.random.fold_in(arg_keys[2], 3), N_PIPE * TOKENS // TOK_DEV)
    routes = jax.vmap(lambda own, number: shared_out(jax.random.fold_in(arg_keys[2], 2), own, number, TOK_DEV, EXPERTS, TOP, CAP, 2))(routes_keys, routes_turns).reshape((N_PIPE, TOKENS, TOP))
    route_probs = jnp.clip(0.1 + 0.5 * jax.random.uniform(arg_keys[3], (N_PIPE, TOKENS, TOP), jnp.float32) ** shard_levels(arg_keys[3], (N_PIPE, TOKENS, TOP), ((0, 8), (1, 32)), -0.2, 0.2), 0.1, 0.6)
    w_in = normal_values(arg_keys[4], (N_PIPE, EXPERTS, D, 2 * FF), D ** -0.5, 0.125, ((0, 8), (1, 32)))
    w_out = normal_values(arg_keys[5], (N_PIPE, EXPERTS, FF, D), FF ** -0.5, 0.3125, ((0, 8), (1, 32)))
    return dict(saved_inputs=saved_inputs, grad_out=grad_out, routes=routes, route_probs=route_probs, w_in=w_in, w_out=w_out)


def silu_parts(gates):
    sigma = jax.nn.sigmoid(gates)
    return gates * sigma, sigma * (1.0 + gates * (1.0 - sigma))


def slot_table(route_ids, route_weights, first, count, capacity):
    tok_count, top_count = route_ids.shape
    flat_ids = route_ids.reshape(-1)
    expert_ids = first + jnp.arange(count, dtype=jnp.int32)
    onehot = (flat_ids[:, None] == expert_ids[None, :]).astype(jnp.int32)
    ranks = jnp.cumsum(onehot, axis=0) - 1
    slots = jnp.sum(onehot * ranks, axis=1)
    local_ids = jnp.sum(onehot * jnp.arange(count, dtype=jnp.int32)[None, :], axis=1)
    hits = jnp.sum(onehot, axis=1)
    dest = jnp.where(hits > 0, local_ids * capacity + slots, count * capacity).astype(jnp.int32)
    token_ids = (jnp.arange(tok_count * top_count, dtype=jnp.int32) // top_count).astype(jnp.int32)
    table = jnp.full((count * capacity + 1,), -1, jnp.int32).at[dest].set(token_ids)[: count * capacity]
    weight = jnp.zeros((count * capacity + 1,), jnp.float32).at[dest].set(route_weights.reshape(-1).astype(jnp.float32))[: count * capacity]
    return table, weight, dest


def pick_rows(input_rows, grad_rows, table, weight):
    valid = table >= 0
    safe_index = jnp.maximum(table, 0)
    picked = jnp.where(valid[:, None], input_rows[safe_index], jnp.zeros((), input_rows.dtype))
    scaled = (weight[:, None] * grad_rows[safe_index].astype(jnp.float32)).astype(jnp.bfloat16)
    return picked, scaled


def expert_grads(expert_in, expert_grad, weight_in, weight_out):
    hidden_units = weight_out.shape[0]
    gate_up = jnp.dot(expert_in, weight_in, preferred_element_type=jnp.float32)
    gates = gate_up[:, :hidden_units]
    upper = gate_up[:, hidden_units:]
    active, slope = silu_parts(gates)
    hidden = (active * upper).astype(jnp.bfloat16)
    hidden_grad = jnp.dot(expert_grad, weight_out.T, preferred_element_type=jnp.float32)
    pre_grad = jnp.concatenate([hidden_grad * upper * slope, hidden_grad * active], axis=1).astype(jnp.bfloat16)
    grad_out_w = jnp.dot(hidden.T, expert_grad, preferred_element_type=jnp.float32).astype(jnp.bfloat16)
    grad_in_w = jnp.dot(expert_in.T, pre_grad, preferred_element_type=jnp.float32).astype(jnp.bfloat16)
    row_grads = jnp.dot(pre_grad, weight_in.T, preferred_element_type=jnp.float32).astype(jnp.bfloat16)
    return row_grads, grad_in_w, grad_out_w


def combine_rows(buffer_rows, dest):
    gathered = buffer_rows[dest].astype(jnp.float32).reshape(-1, TOP, buffer_rows.shape[1])
    return jnp.sum(gathered, axis=1)


def one_section(packed):
    section_in, section_grad, section_routes, section_probs, weight_in, weight_out = packed
    block_in = section_in.reshape(N_EXPERT, TOK_DEV, D)
    block_grad = section_grad.reshape(N_EXPERT, TOK_DEV, D)
    tables, weights, dests = jax.vmap(lambda ids, probs: slot_table(ids, probs, 0, EXPERTS, CAP))(
        section_routes.reshape(N_EXPERT, TOK_DEV, TOP), section_probs.reshape(N_EXPERT, TOK_DEV, TOP))
    rows_in, rows_grad = jax.vmap(pick_rows)(block_in, block_grad, tables, weights)
    rows_in = rows_in.reshape(N_EXPERT, EXPERTS, CAP, D).transpose(1, 0, 2, 3).reshape(EXPERTS, N_EXPERT * CAP, D)
    rows_grad = rows_grad.reshape(N_EXPERT, EXPERTS, CAP, D).transpose(1, 0, 2, 3).reshape(EXPERTS, N_EXPERT * CAP, D)
    row_grads, grad_in_w, grad_out_w = lax.map(lambda items: expert_grads(*items), (rows_in, rows_grad, weight_in, weight_out))
    row_grads = row_grads.reshape(EXPERTS, N_EXPERT, CAP, D).transpose(1, 0, 2, 3).reshape(N_EXPERT, EXPERTS * CAP, D)
    token_grads = jax.vmap(combine_rows)(row_grads, dests)
    return token_grads.reshape(TOKENS, D), grad_in_w, grad_out_w


def reference(saved_inputs, grad_out, routes, route_probs, w_in, w_out):
    section_inputs = saved_inputs[::-1]
    grad_tokens, grad_w_in, grad_w_out = lax.map(one_section, (section_inputs, grad_out, routes, route_probs, w_in, w_out))
    return grad_tokens, grad_w_in, grad_w_out
```

```python
import functools
import jax
import jax.numpy as jnp
from jax import lax
from jax.experimental import pallas as pl
from jax.experimental.pallas import tpu as pltpu
from jax.sharding import PartitionSpec as P

CAP = 36
XN = 4
ZN = 8
TOK = 128
F32 = jnp.float32
BF16 = jnp.bfloat16
VMEM_LIMIT = 40 * 1024 * 1024


def round_up(value, unit):
    return -(-value // unit) * unit


def call(kernel, out_shapes, args, flops, moved, smem=()):
    specs = [
        pl.BlockSpec(memory_space=pltpu.SMEM if i in smem else pltpu.VMEM) for i in range(len(args))
    ]
    return pl.pallas_call(
        kernel,
        out_shape=out_shapes,
        in_specs=specs,
        out_specs=[pl.BlockSpec(memory_space=pltpu.VMEM)] * len(out_shapes),
        compiler_params=pltpu.CompilerParams(vmem_limit_bytes=VMEM_LIMIT),
        cost_estimate=pl.CostEstimate(flops=flops, bytes_accessed=moved, transcendentals=0),
    )(*args)


def columns(pieces, low, high):
    start = 0
    for ref in pieces:
        stop = start + ref.shape[1]
        if start <= low and high <= stop:
            return ref[:, low - start : high - start]
        start = stop
    raise ValueError


def group(refs, counts):
    out, at = [], 0
    for count in counts:
        out.append(refs[at : at + count])
        at += count
    return out, refs[at:]


def tiles(width):
    return [(low, low + 512) for low in range(0, width, 512)]


def pick_grad_kernel(counts, send, slot, width, ids_ref, *refs):
    blocks, refs = group(refs, counts)
    outs, sel_ref = refs[:XN], refs[XN]
    meta = jnp.concatenate(
        [columns(b, width, width + TOK)[0:32, :].astype(F32) for b in blocks], axis=1
    )
    total = meta.shape[1]
    ids = meta[0:8]
    probs = meta[8:16] + meta[16:24] + meta[24:32]
    marks, weights = [], []
    for j in range(XN):
        hit = ids == ids_ref[0, j].astype(F32)
        marks.append(jnp.sum(jnp.where(hit, 1.0, 0.0), axis=0, keepdims=True))
        weights.append(jnp.sum(jnp.where(hit, probs, 0.0), axis=0, keepdims=True))
    mark = jnp.concatenate(marks + [jnp.zeros((8 - XN, total), F32)], axis=0)
    earlier = lax.broadcasted_iota(jnp.int32, (total, total), 0) < lax.broadcasted_iota(
        jnp.int32, (total, total), 1
    )
    rank = jnp.dot(
        mark.astype(BF16), jnp.where(earlier, 1.0, 0.0).astype(BF16), preferred_element_type=F32
    )
    place = lax.broadcasted_iota(jnp.int32, (slot, total), 0).astype(F32)
    scales = []
    for j in range(XN):
        wanted = jnp.where(mark[j : j + 1] > 0.5, rank[j : j + 1], -1.0)
        chosen = place == wanted
        sel_ref[j * slot : (j + 1) * slot, :] = jnp.where(chosen, 1.0, 0.0).astype(BF16)
        scales.append(jnp.sum(jnp.where(chosen, weights[j], 0.0), axis=1, keepdims=True))
    scale = jnp.concatenate(scales, axis=0)
    for low, high in tiles(width):
        rows = sum(
            jnp.dot(
                sel_ref[:, i * TOK : (i + 1) * TOK],
                columns(b, low, high),
                preferred_element_type=F32,
            )
            for i, b in enumerate(blocks)
        )
        rows = (rows * scale).astype(BF16)
        for j in range(XN):
            outs[j][:, low:high] = rows[j * slot : j * slot + send]


def pick_in_kernel(counts, send, slot, width, sel_ref, *refs):
    blocks, outs = group(refs, counts)
    for low, high in tiles(width):
        rows = sum(
            jnp.dot(
                sel_ref[:, i * TOK : (i + 1) * TOK],
                columns(b, low, high),
                preferred_element_type=F32,
            )
            for i, b in enumerate(blocks)
        ).astype(BF16)
        for j in range(XN):
            outs[j][:, low:high] = rows[j * slot : j * slot + send]


def stack_rows(dst, parts, send, slot):
    for j, part in enumerate(parts):
        dst[(j + 1) * slot - 16 : (j + 1) * slot, :] = jnp.zeros((16, dst.shape[1]), dst.dtype)
        dst[j * slot : j * slot + send, :] = part[...]


def expert_kernel(send, slot, *refs):
    grads, ins = refs[:XN], refs[XN : 2 * XN]
    w_in, w_out = refs[2 * XN : 2 * XN + 2]
    refs = refs[2 * XN + 2 :]
    backs, (x_ref, g_ref, hidden_ref, pre_ref) = refs[:XN], refs[XN:]
    units, width = w_out.shape
    stack_rows(x_ref, ins, send, slot)
    stack_rows(g_ref, grads, send, slot)
    step = 128
    for low in range(0, units, step):
        gate = jnp.dot(x_ref[...], w_in[:, low : low + step], preferred_element_type=F32)
        upper = jnp.dot(
            x_ref[...], w_in[:, units + low : units + low + step], preferred_element_type=F32
        )
        back = lax.dot_general(
            g_ref[...],
            w_out[low : low + step, :],
            (((1,), (1,)), ((), ())),
            preferred_element_type=F32,
        )
        sigma = 1.0 / (1.0 + jnp.exp(-gate))
        active = gate * sigma
        slope = sigma * (1.0 + gate * (1.0 - sigma))
        hidden_ref[:, low : low + step] = (active * upper).astype(BF16)
        pre_ref[:, low : low + step] = (back * upper * slope).astype(BF16)
        pre_ref[:, units + low : units + low + step] = (back * active).astype(BF16)
    for low, high in tiles(width):
        rows = lax.dot_general(
            pre_ref[...], w_in[low:high, :], (((1,), (1,)), ((), ())), preferred_element_type=F32
        ).astype(BF16)
        for j in range(XN):
            backs[j][:, low:high] = rows[j * slot : j * slot + send]


def combine_kernel(send, slot, width, adds, outs_at, sel_ref, *refs):
    backs, refs = refs[:XN], refs[XN:]
    incoming, refs = refs[: len(adds)], refs[len(adds) :]
    outs, stacked = refs[:-1], refs[-1]
    stack_rows(stacked, backs, send, slot)
    for out, (block, first) in zip(outs, outs_at):
        for low, high in tiles(out.shape[1]):
            total = lax.dot_general(
                sel_ref[:, block * TOK : (block + 1) * TOK],
                stacked[:, first + low : first + high],
                (((0,), (0,)), ((), ())),
                preferred_element_type=F32,
            )
            for ref, (owner, start) in zip(incoming, adds):
                at = first + low - start
                if owner == block and 0 <= at and at + 512 <= ref.shape[1]:
                    total = total + ref[:, at : at + 512].astype(F32)
            out[:, low:high] = total.astype(out.dtype)


def combine(send, slot, width, sel, backs, incoming, adds, outs_at, out_shapes):
    rows = sel.shape[0]
    args = [sel, *backs, *incoming]
    return pl.pallas_call(
        functools.partial(combine_kernel, send, slot, width, adds, outs_at),
        out_shape=out_shapes,
        in_specs=[pl.BlockSpec(memory_space=pltpu.VMEM)] * len(args),
        out_specs=[pl.BlockSpec(memory_space=pltpu.VMEM)] * len(out_shapes),
        scratch_shapes=[pltpu.VMEM((rows, width), BF16)],
        compiler_params=pltpu.CompilerParams(vmem_limit_bytes=VMEM_LIMIT),
        cost_estimate=pl.CostEstimate(
            flops=2 * rows * sel.shape[1] * width, bytes_accessed=rows * width * 4, transcendentals=0
        ),
    )(*args)


def weight_kernel(count, *refs):
    xs, gs, hs, ps = (refs[i * count : (i + 1) * count] for i in range(4))
    in_ref, out_ref = refs[4 * count :]
    dims = (((0,), (0,)), ((), ()))
    in_ref[...] = sum(
        lax.dot_general(x[...], p[...], dims, preferred_element_type=F32) for x, p in zip(xs, ps)
    ).astype(BF16)
    out_ref[...] = sum(
        lax.dot_general(h[...], g[...], dims, preferred_element_type=F32) for h, g in zip(hs, gs)
    ).astype(BF16)


def weight_grads(xs, gs, hs, ps, width, units):
    count = len(xs)
    tile = 256
    cut = [pl.BlockSpec((a.shape[0], tile), lambda i: (0, i)) for a in xs + gs]
    whole = [pl.BlockSpec(a.shape, lambda i: (0, 0)) for a in hs + ps]
    rows = sum(a.shape[0] for a in xs)
    return pl.pallas_call(
        functools.partial(weight_kernel, count),
        grid=(width // tile,),
        in_specs=cut + whole,
        out_specs=[
            pl.BlockSpec((tile, 2 * units), lambda i: (i, 0)),
            pl.BlockSpec((units, tile), lambda i: (0, i)),
        ],
        out_shape=[
            jax.ShapeDtypeStruct((width, 2 * units), BF16),
            jax.ShapeDtypeStruct((units, width), BF16),
        ],
        compiler_params=pltpu.CompilerParams(vmem_limit_bytes=VMEM_LIMIT),
        cost_estimate=pl.CostEstimate(
            flops=6 * rows * units * width, bytes_accessed=rows * width * 6, transcendentals=0
        ),
    )(*xs, *gs, *hs, *ps)


def along_x(block, shift):
    pairs = [
        (x * ZN + z, (x + shift) % XN * ZN + z) for x in range(XN) for z in range(ZN)
    ]
    return lax.ppermute(block, "expert", pairs)


def along_z(block, shift):
    pairs = [
        (x * ZN + z, x * ZN + (z + shift) % ZN) for x in range(XN) for z in range(ZN)
    ]
    return lax.ppermute(block, "expert", pairs)


def pad_rows(block, rows):
    return jnp.pad(block, ((0, rows - block.shape[0]), (0, 0)))


def payload(grads, routes, probs):
    first = lax.reduce_precision(probs, 8, 7)
    rest = probs - first
    second = lax.reduce_precision(rest, 8, 7)
    third = rest - second
    table = jnp.concatenate([routes.astype(F32), first, second, third], axis=1)
    meta = pad_rows(table.T, TOK).astype(BF16)
    return jnp.concatenate([grads, meta], axis=1)


def per_device(saved_inputs, grad_out, routes, route_probs, w_in, w_out):
    sections = lax.axis_size("pipe")
    width = saved_inputs.shape[2]
    half = width // 2
    weight_in, weight_out = w_in[0, 0], w_out[0, 0]
    units = weight_out.shape[0]
    place = lax.axis_index("expert")
    column, depth = place // ZN, place % ZN
    ids = ((column + jnp.arange(XN, dtype=jnp.int32)) % XN * ZN + depth)[None, :]

    relayed = lax.ppermute(
        saved_inputs[0], "pipe", [(i, sections - 1 - i) for i in range(sections)]
    )
    pay = payload(grad_out[0], routes[0], route_probs[0])

    def travel(own):
        steps = [[(own,)]]
        up, down = own, own
        for _ in range(ZN // 2 - 1):
            up, down = along_z(up, 1), along_z(down, -1)
            steps.append([(up,), (down,)])
        steps.append([(along_z(up[:, :half], 1), along_z(down[:, half:], -1))])
        return steps

    grad_steps, in_steps = travel(pay), travel(relayed)
    chunks = []
    for grad_blocks, in_blocks in zip(grad_steps, in_steps):
        count = len(grad_blocks)
        cap = CAP * count
        send, slot = round_up(cap, 8), round_up(cap, 16)
        total = count * TOK
        rows = jax.ShapeDtypeStruct((send, width), BF16)
        flops = 2 * XN * slot * total * width
        moved = (XN * slot + total) * width * 2
        flat = [ref for b in grad_blocks for ref in b]
        *picked_grad, sel = call(
            functools.partial(
                pick_grad_kernel, tuple(len(b) for b in grad_blocks), send, slot, width
            ),
            [rows] * XN + [jax.ShapeDtypeStruct((XN * slot, total), BF16)],
            [ids, *flat],
            flops,
            moved,
            smem=(0,),
        )
        flat = [ref for b in in_blocks for ref in b]
        picked_in = call(
            functools.partial(pick_in_kernel, tuple(len(b) for b in in_blocks), send, slot, width),
            [rows] * XN,
            [sel, *flat],
            flops,
            moved,
        )
        got_grad = [picked_grad[0]] + [along_x(picked_grad[j], j) for j in range(1, XN)]
        got_in = [picked_in[0]] + [along_x(picked_in[j], j) for j in range(1, XN)]
        chunks.append((send, slot, sel, got_grad, got_in))

    done = []
    for send, slot, sel, got_grad, got_in in chunks:
        all_rows = XN * slot
        shape = jax.ShapeDtypeStruct
        *backs, x_rows, g_rows, hidden, pre = call(
            functools.partial(expert_kernel, send, slot),
            [shape((send, width), BF16)] * XN
            + [shape((all_rows, width), BF16)] * 2
            + [shape((all_rows, units), BF16), shape((all_rows, 2 * units), BF16)],
            [*got_grad, *got_in, weight_in, weight_out],
            10 * all_rows * units * width,
            all_rows * width * 8,
        )
        returned = [backs[0]] + [along_x(backs[j], -j) for j in range(1, XN)]
        done.append((send, slot, sel, returned, x_rows, g_rows, hidden, pre))

    grad_w_in, grad_w_out = weight_grads(
        *([c[i] for c in done] for i in (4, 5, 6, 7)), width, units
    )

    part = jax.ShapeDtypeStruct((TOK, half), BF16)
    full = jax.ShapeDtypeStruct((TOK, width), BF16)
    incoming, adds = [], ()
    for index in range(len(done) - 1, -1, -1):
        send, slot, sel, returned = done[index][:4]
        if index == len(done) - 1:
            outs_at, shapes = ((0, 0), (0, half)), [part, part]
        elif index > 0:
            outs_at, shapes = ((0, 0), (1, 0)), [full, full]
        else:
            outs_at, shapes = ((0, 0),), [jax.ShapeDtypeStruct((TOK, width), F32)]
            adds = ((0, 0), (0, 0))
        sums = combine(send, slot, width, sel, returned, incoming, adds, outs_at, shapes)
        if index > 0:
            incoming = [along_z(sums[0], -1), along_z(sums[1], 1)]
            adds = ((0, 0), (1, half)) if index == len(done) - 1 else ((0, 0), (1, 0))
    return sums[0][None], grad_w_in[None, None], grad_w_out[None, None]


def solution(mesh):
    rows = P("pipe", "expert", None)
    weights = P("pipe", "expert", None, None)
    return jax.shard_map(
        per_device,
        mesh=mesh,
        in_specs=(rows, rows, rows, rows, weights, weights),
        out_specs=(rows, weights, weights),
        check_vma=False,
    )
```

```python
import functools
import jax
import jax.numpy as jnp
from jax import lax
from jax.experimental import pallas as pl
from jax.experimental.pallas import tpu as pltpu
from jax.sharding import PartitionSpec as P

CAP = 36
XN = 4
ZN = 8
TOK = 128
TILE = 512
F32 = jnp.float32
BF16 = jnp.bfloat16
VMEM_LIMIT = 16 * 1024 * 1024
VMEM = pl.BlockSpec(memory_space=pltpu.VMEM)
NT = (((1,), (1,)), ((), ()))
TN = (((0,), (0,)), ((), ()))


def round_up(value, unit):
    return -(-value // unit) * unit


def shaped(rows, width, kind=BF16):
    return jax.ShapeDtypeStruct((rows, width), kind)


def run(kernel, outs, args, flops, moved, scratch=(), smem=0):
    specs = [pl.BlockSpec(memory_space=pltpu.SMEM)] * smem + [VMEM] * (len(args) - smem)
    return pl.pallas_call(
        kernel,
        out_shape=outs,
        in_specs=specs,
        out_specs=[VMEM] * len(outs),
        scratch_shapes=scratch,
        compiler_params=pltpu.CompilerParams(vmem_limit_bytes=VMEM_LIMIT),
        cost_estimate=pl.CostEstimate(flops=flops, bytes_accessed=moved, transcendentals=0),
    )(*args)


def each_tile(count, size, step):
    def body(i, carry):
        step(pl.multiple_of(i * size, size))
        return carry

    lax.fori_loop(0, count, body, 0)


def select_rows(ids_ref, meta, slot, sel_ref):
    total = meta.shape[1]
    ids = meta[0:8]
    probs = meta[8:16] + meta[16:24] + meta[24:32]
    marks, weights = [], []
    for j in range(XN):
        hit = ids == ids_ref[0, j].astype(F32)
        marks.append(jnp.sum(jnp.where(hit, 1.0, 0.0), axis=0, keepdims=True))
        weights.append(jnp.sum(jnp.where(hit, probs, 0.0), axis=0, keepdims=True))
    mark = jnp.concatenate(marks + [jnp.zeros((8 - XN, total), F32)], axis=0)
    earlier = lax.broadcasted_iota(jnp.int32, (total, total), 0) < lax.broadcasted_iota(
        jnp.int32, (total, total), 1
    )
    rank = jnp.dot(
        mark.astype(BF16), jnp.where(earlier, 1.0, 0.0).astype(BF16), preferred_element_type=F32
    )
    place = lax.broadcasted_iota(jnp.int32, (slot, total), 0).astype(F32)
    scales = []
    for j in range(XN):
        wanted = jnp.where(mark[j : j + 1] > 0.5, rank[j : j + 1], -1.0)
        chosen = place == wanted
        sel_ref[j * slot : (j + 1) * slot, :] = jnp.where(chosen, 1.0, 0.0).astype(BF16)
        scales.append(jnp.sum(jnp.where(chosen, weights[j], 0.0), axis=1, keepdims=True))
    return jnp.concatenate(scales, axis=0)


def pick_kernel(sizes, width, grads, ins, known, *refs):
    send, slot = sizes
    refs = list(refs)
    ids_ref = refs.pop(0) if grads else None
    in_sel = refs.pop(0) if known else None
    sel_ref = refs.pop() if grads else None
    outs, refs = refs[-XN:], refs[:-XN]
    scale = None
    if grads:
        meta = jnp.concatenate(
            [refs[i][0:32, at + width : at + width + TOK].astype(F32) for i, at in grads], axis=1
        )
        scale = select_rows(ids_ref, meta, slot, sel_ref)
    parts = []
    if grads:
        parts.append((grads, sel_ref, scale, 0))
    if ins:
        parts.append((ins, in_sel if known else sel_ref, None, width if grads else 0))
    for blocks, sel, factor, base in parts:

        def step(low):
            rows = sum(
                jnp.dot(
                    sel[:, n * TOK : (n + 1) * TOK],
                    refs[i][:, pl.ds(pl.multiple_of(at + low, TOK), TILE)],
                    preferred_element_type=F32,
                )
                for n, (i, at) in enumerate(blocks)
            )
            if factor is not None:
                rows = rows * factor
            rows = rows.astype(BF16)
            for j in range(XN):
                outs[j][:, pl.ds(pl.multiple_of(base + low, TOK), TILE)] = rows[
                    j * slot : j * slot + send
                ]

        each_tile(width // TILE, TILE, step)


def pick(sizes, width, ids, grads=(), ins=(), sel=None):
    arrays, places = [], []
    for blocks in (grads, ins):
        found = []
        for array, at in blocks:
            index = next((i for i, a in enumerate(arrays) if a is array), None)
            if index is None:
                index = len(arrays)
                arrays.append(array)
            found.append((index, at))
        places.append(tuple(found))
    send, slot = sizes
    count = max(len(grads), len(ins))
    halves = bool(grads) + bool(ins)
    outs = [shaped(send, width * halves)] * XN
    args = list(arrays)
    if sel is not None:
        args = [sel] + args
    if grads:
        args = [ids] + args
        outs = outs + [shaped(XN * slot, count * TOK)]
    return run(
        functools.partial(pick_kernel, sizes, width, *places, sel is not None),
        outs,
        args,
        2 * XN * slot * count * TOK * width * halves,
        XN * slot * width * 4 * halves,
        smem=1 if grads else 0,
    )


def stack_rows(dst, parts, sizes, at):
    send, slot = sizes
    width = dst.shape[1]
    for j, part in enumerate(parts):
        dst[(j + 1) * slot - 16 : (j + 1) * slot, :] = jnp.zeros((16, width), dst.dtype)
        dst[j * slot : j * slot + send, :] = part[:, at : at + width]


def expert_kernel(sizes, grad_at, in_at, shared, *refs):
    send, slot = sizes
    grads, refs = refs[:XN], refs[XN:]
    ins = grads if shared else refs[:XN]
    refs = refs if shared else refs[XN:]
    w_in, w_out = refs[:2]
    backs, (x_ref, g_ref, hidden_ref, pre_ref) = refs[2 : 2 + XN], refs[2 + XN :]
    units, width = w_out.shape
    stack_rows(x_ref, ins, sizes, in_at)
    stack_rows(g_ref, grads, sizes, grad_at)

    def forward(low):
        high = pl.multiple_of(units + low, TOK)
        pair = jnp.concatenate([w_in[:, pl.ds(low, TOK)], w_in[:, pl.ds(high, TOK)]], axis=1)
        both = jnp.dot(x_ref[...], pair, preferred_element_type=F32)
        gate, upper = both[:, :TOK], both[:, TOK:]
        back = lax.dot_general(
            g_ref[...], w_out[pl.ds(low, TOK), :], NT, preferred_element_type=F32
        )
        sigma = 1.0 / (1.0 + jnp.exp(-gate))
        active = gate * sigma
        slope = sigma * (1.0 + gate * (1.0 - sigma))
        hidden_ref[:, pl.ds(low, TOK)] = (active * upper).astype(BF16)
        pre_ref[:, pl.ds(low, TOK)] = (back * upper * slope).astype(BF16)
        pre_ref[:, pl.ds(high, TOK)] = (back * active).astype(BF16)

    each_tile(units // TOK, TOK, forward)

    def backward(low):
        rows = lax.dot_general(
            pre_ref[...], w_in[pl.ds(low, TILE), :], NT, preferred_element_type=F32
        ).astype(BF16)
        for j in range(XN):
            backs[j][:, pl.ds(low, TILE)] = rows[j * slot : j * slot + send]

    each_tile(width // TILE, TILE, backward)


def expert(sizes, grads, grad_at, ins, in_at, w_in, w_out):
    send, slot = sizes
    units, width = w_out.shape
    shared = grads is ins
    rows = XN * slot
    return run(
        functools.partial(expert_kernel, sizes, grad_at, in_at, shared),
        [shaped(send, width)] * XN
        + [shaped(rows, width)] * 2
        + [shaped(rows, units), shaped(rows, 2 * units)],
        [*grads, *(() if shared else ins), w_in, w_out],
        10 * rows * units * width,
        rows * width * 8,
    )


def combine_kernel(sizes, adds, outs_at, sel_ref, *refs):
    backs, refs = refs[:XN], refs[XN:]
    incoming, refs = refs[: len(adds)], refs[len(adds) :]
    outs, stacked = refs[:-1], refs[-1]
    stack_rows(stacked, backs, sizes, 0)
    for out, (block, first) in zip(outs, outs_at):
        for low in range(0, out.shape[1], TILE):
            total = lax.dot_general(
                sel_ref[:, block * TOK : (block + 1) * TOK],
                stacked[:, first + low : first + low + TILE],
                TN,
                preferred_element_type=F32,
            )
            for ref, (owner, start) in zip(incoming, adds):
                at = first + low - start
                if owner == block and 0 <= at and at + TILE <= ref.shape[1]:
                    total = total + ref[:, at : at + TILE].astype(F32)
            out[:, low : low + TILE] = total.astype(out.dtype)


def combine(sizes, sel, backs, incoming, adds, outs_at, outs):
    rows, total = sel.shape
    width = backs[0].shape[1]
    return run(
        functools.partial(combine_kernel, sizes, adds, outs_at),
        outs,
        [sel, *backs, *incoming],
        2 * rows * total * width,
        rows * width * 4,
        scratch=[pltpu.VMEM((rows, width), BF16)],
    )


def weight_kernel(count, turned, *refs):
    out = refs[-1]
    total = sum(
        lax.dot_general(a[...], b[...], TN, preferred_element_type=F32)
        for a, b in zip(refs[:count], refs[count : 2 * count])
    )
    out[...] = (total.T if turned else total).astype(BF16)


def weight_grads(wide, narrow, turned):
    tile = 256
    count = len(wide)
    width, units = wide[0].shape[1], narrow[0].shape[1]
    rows = sum(a.shape[0] for a in wide)
    return pl.pallas_call(
        functools.partial(weight_kernel, count, turned),
        grid=(width // tile,),
        in_specs=[pl.BlockSpec((a.shape[0], tile), lambda i: (0, i)) for a in wide]
        + [pl.BlockSpec(a.shape, lambda i: (0, 0)) for a in narrow],
        out_specs=pl.BlockSpec((units, tile), lambda i: (0, i))
        if turned
        else pl.BlockSpec((tile, units), lambda i: (i, 0)),
        out_shape=shaped(units, width) if turned else shaped(width, units),
        compiler_params=pltpu.CompilerParams(vmem_limit_bytes=VMEM_LIMIT),
        cost_estimate=pl.CostEstimate(
            flops=2 * rows * units * width, bytes_accessed=rows * width * 2, transcendentals=0
        ),
    )(*wide, *narrow)


def along_x(parts, sign):
    moved = [parts[0]]
    for j in range(1, XN):
        pairs = [
            (x * ZN + z, (x + sign * j) % XN * ZN + z) for x in range(XN) for z in range(ZN)
        ]
        moved.append(lax.ppermute(parts[j], "expert", pairs))
    return moved


def along_z(block, shift):
    pairs = [(x * ZN + z, x * ZN + (z + shift) % ZN) for x in range(XN) for z in range(ZN)]
    return lax.ppermute(block, "expert", pairs)


def payload(grads, routes, probs):
    first = lax.reduce_precision(probs, 8, 7)
    rest = probs - first
    second = lax.reduce_precision(rest, 8, 7)
    third = rest - second
    table = jnp.concatenate([routes.astype(F32), first, second, third], axis=1).T
    meta = jnp.pad(table, ((0, TOK - table.shape[0]), (0, 0))).astype(BF16)
    return jnp.concatenate([grads, meta], axis=1)


def per_device(saved_inputs, grad_out, routes, route_probs, w_in, w_out):
    sections = lax.axis_size("pipe")
    width = saved_inputs.shape[2]
    half = width // 2
    over = width + TOK
    weight_in, weight_out = w_in[0, 0], w_out[0, 0]
    place = lax.axis_index("expert")
    column, depth = place // ZN, place % ZN
    ids = ((column + jnp.arange(XN, dtype=jnp.int32)) % XN * ZN + depth)[None, :]
    sizes = [
        (round_up(CAP * n, 8), round_up(CAP * n, 16)) for n in (1, 2, 2, 2, 1)
    ]

    own = lax.ppermute(saved_inputs[0], "pipe", [(i, sections - 1 - i) for i in range(sections)])
    pay = payload(grad_out[0], routes[0], route_probs[0])
    up1, down1 = along_z(pay, 1), along_z(pay, -1)
    *rows, sel0 = pick(sizes[0], width, ids, grads=[(pay, 0)])
    g0 = along_x(rows, 1)
    rows = pick(sizes[0], width, ids, ins=[(own, 0)], sel=sel0)
    i0 = along_x(rows, 1)
    up2 = along_z(jnp.concatenate([up1, own], axis=1), 1)
    down2 = along_z(jnp.concatenate([down1, own], axis=1), -1)
    *rows, sel1 = pick(sizes[1], width, ids, grads=[(up1, 0), (down1, 0)])
    g1 = along_x(rows, 1)
    up3, down3 = along_z(up2, 1), along_z(down2, -1)
    *rows, sel2 = pick(
        sizes[2], width, ids, [(up2, 0), (down2, 0)], [(up2, over), (down2, over)], sel1
    )
    g2i1 = along_x(rows, 1)
    up4 = along_z(up3, 1)
    down4 = along_z(down3[:, over:], -1)
    *rows, sel3 = pick(
        sizes[3], width, ids, [(up3, 0), (down3, 0)], [(up3, over), (down3, over)], sel2
    )
    g3i2 = along_x(rows, 1)
    down5 = along_z(down4, -1)
    *rows, sel4 = pick(sizes[4], width, ids, [(up4, 0)], [(down5, 0)])
    g4i4 = along_x(rows, 1)
    rows = pick(sizes[3], width, ids, ins=[(up4, over), (down4, 0)], sel=sel3)
    i3 = along_x(rows, 1)

    sels = [sel0, sel1, sel2, sel3, sel4]
    feeds = [
        (g0, 0, i0, 0),
        (g1, 0, g2i1, width),
        (g2i1, 0, g3i2, width),
        (g3i2, 0, i3, 0),
        (g4i4, 0, g4i4, width),
    ]
    held, returned = [], []
    for n, feed in enumerate(feeds):
        *backs, x_rows, g_rows, hidden, pre = expert(sizes[n], *feed, weight_in, weight_out)
        held.append((x_rows, g_rows, hidden, pre))
        returned.append(along_x(backs, -1))
    xs, gs, hs, ps = zip(*held)
    grad_w_in = weight_grads(xs, ps, False)
    grad_w_out = weight_grads(gs, hs, True)

    part, full = shaped(TOK, half), shaped(TOK, width)
    down, up = combine(sizes[4], sel4, returned[4], [], (), ((0, 0), (0, half)), [part, part])
    adds = ((0, 0), (1, half))
    for n in (3, 2, 1):
        incoming = [along_z(down, -1), along_z(up, 1)]
        down, up = combine(
            sizes[n], sels[n], returned[n], incoming, adds, ((0, 0), (1, 0)), [full, full]
        )
        adds = ((0, 0), (1, 0))
    incoming = [along_z(down, -1), along_z(up, 1)]
    (tokens,) = combine(
        sizes[0],
        sel0,
        returned[0],
        incoming,
        ((0, 0), (0, 0)),
        ((0, 0),),
        [shaped(TOK, width, F32)],
    )
    return tokens[None], grad_w_in[None, None], grad_w_out[None, None]


def solution(mesh):
    rows = P("pipe", "expert", None)
    weights = P("pipe", "expert", None, None)
    return jax.shard_map(
        per_device,
        mesh=mesh,
        in_specs=(rows, rows, rows, rows, weights, weights),
        out_specs=(rows, weights, weights),
        check_vma=False,
    )
```

```python
import functools
import jax
import jax.numpy as jnp
from jax import lax
from jax.experimental import pallas as pl
from jax.experimental.pallas import tpu as pltpu
from jax.sharding import PartitionSpec as P

CAP = 36
XN = 4
ZN = 8
TOK = 128
TILE = 512
HALF = 256
F32 = jnp.float32
BF16 = jnp.bfloat16
VMEM_LIMIT = 16 * 1024 * 1024
VMEM = pl.BlockSpec(memory_space=pltpu.VMEM)
NT = (((1,), (1,)), ((), ()))
TN = (((0,), (0,)), ((), ()))


def round_up(value, unit):
    return -(-value // unit) * unit


def shaped(rows, width, kind=BF16):
    return jax.ShapeDtypeStruct((rows, width), kind)


def run(kernel, outs, args, flops, moved, scratch=(), smem=0):
    specs = [pl.BlockSpec(memory_space=pltpu.SMEM)] * smem + [VMEM] * (len(args) - smem)
    return pl.pallas_call(
        kernel,
        out_shape=outs,
        in_specs=specs,
        out_specs=[VMEM] * len(outs),
        scratch_shapes=scratch,
        compiler_params=pltpu.CompilerParams(vmem_limit_bytes=VMEM_LIMIT),
        cost_estimate=pl.CostEstimate(flops=flops, bytes_accessed=moved, transcendentals=0),
    )(*args)


def each_tile(count, size, step):
    def body(i, carry):
        step(pl.multiple_of(i * size, size))
        return carry

    lax.fori_loop(0, count, body, 0)


def select_rows(ids_ref, meta, slot, sel_ref):
    total = meta.shape[1]
    ids = meta[0:8]
    probs = meta[8:16] + meta[16:24] + meta[24:32]
    marks, weights = [], []
    for j in range(XN):
        hit = ids == ids_ref[0, j].astype(F32)
        marks.append(jnp.sum(jnp.where(hit, 1.0, 0.0), axis=0, keepdims=True))
        weights.append(jnp.sum(jnp.where(hit, probs, 0.0), axis=0, keepdims=True))
    mark = jnp.concatenate(marks + [jnp.zeros((8 - XN, total), F32)], axis=0)
    earlier = lax.broadcasted_iota(jnp.int32, (total, total), 0) < lax.broadcasted_iota(
        jnp.int32, (total, total), 1
    )
    rank = jnp.dot(
        mark.astype(BF16), jnp.where(earlier, 1.0, 0.0).astype(BF16), preferred_element_type=F32
    )
    place = lax.broadcasted_iota(jnp.int32, (slot, total), 0).astype(F32)
    scales = []
    for j in range(XN):
        wanted = jnp.where(mark[j : j + 1] > 0.5, rank[j : j + 1], -1.0)
        chosen = place == wanted
        sel_ref[j * slot : (j + 1) * slot, :] = jnp.where(chosen, 1.0, 0.0).astype(BF16)
        scales.append(jnp.sum(jnp.where(chosen, weights[j], 0.0), axis=1, keepdims=True))
    return jnp.concatenate(scales, axis=0)


def pick_kernel(sizes, width, grads, ins, ids_ref, *refs):
    send, slot = sizes
    refs, outs, sel_ref = refs[: -XN - 1], refs[-XN - 1 : -1], refs[-1]
    meta = jnp.concatenate(
        [refs[i][0:32, at + width : at + width + TOK].astype(F32) for i, at in grads], axis=1
    )
    scale = select_rows(ids_ref, meta, slot, sel_ref)
    over = width + TOK
    shared = all(i == k and at + over == to for (i, at), (k, to) in zip(grads, ins))

    def move(blocks, take, put, factor):
        rows = sum(
            jnp.dot(
                sel_ref[:, n * TOK : (n + 1) * TOK],
                refs[i][:, pl.ds(pl.multiple_of(at + take, TOK), TILE)],
                preferred_element_type=F32,
            )
            for n, (i, at) in enumerate(blocks)
        )
        if factor is not None:
            rows = rows * factor
        rows = rows.astype(BF16)
        for j in range(XN):
            outs[j][:, pl.ds(pl.multiple_of(put, TOK), TILE)] = rows[j * slot : j * slot + send]

    if shared:

        def both(low):
            second = (low >= width).astype(jnp.int32)
            factor = jnp.where(low >= width, jnp.ones_like(scale), scale)
            move(grads, low + second * TOK, low, factor)

        each_tile(2 * width // TILE, TILE, both)
    else:
        each_tile(width // TILE, TILE, lambda low: move(grads, low, low, scale))
        each_tile(width // TILE, TILE, lambda low: move(ins, low, width + low, None))


def pick(sizes, width, ids, grads, ins):
    arrays, places = [], []
    for blocks in (grads, ins):
        found = []
        for array, at in blocks:
            index = next((i for i, a in enumerate(arrays) if a is array), None)
            if index is None:
                index = len(arrays)
                arrays.append(array)
            found.append((index, at))
        places.append(tuple(found))
    send, slot = sizes
    total = len(grads) * TOK
    *rows, sel = run(
        functools.partial(pick_kernel, sizes, width, *places),
        [shaped(send, 2 * width)] * XN + [shaped(XN * slot, total)],
        [ids, *arrays],
        4 * XN * slot * total * width,
        XN * slot * width * 8,
        smem=1,
    )
    return rows, sel


def stack_rows(dst, parts, sizes, base):
    send, slot = sizes

    def step(low):
        for j, part in enumerate(parts):
            dst[(j + 1) * slot - 16 : (j + 1) * slot, pl.ds(low, TILE)] = jnp.zeros(
                (16, TILE), dst.dtype
            )
            dst[j * slot : j * slot + send, pl.ds(low, TILE)] = part[
                :, pl.ds(pl.multiple_of(base + low, TOK), TILE)
            ]

    each_tile(dst.shape[1] // TILE, TILE, step)


def expert_kernel(sizes, *refs):
    send, slot = sizes
    rows, (w_in, w_out) = refs[:XN], refs[XN : XN + 2]
    backs, (x_ref, g_ref, hidden_ref, pre_ref) = refs[XN + 2 : 2 * XN + 2], refs[2 * XN + 2 :]
    units, width = w_out.shape
    stack_rows(x_ref, rows, sizes, width)
    stack_rows(g_ref, rows, sizes, 0)

    def forward(low):
        high = pl.multiple_of(units + low, TOK)
        pair = jnp.concatenate([w_in[:, pl.ds(low, TOK)], w_in[:, pl.ds(high, TOK)]], axis=1)
        both = jnp.dot(x_ref[...], pair, preferred_element_type=F32)
        gate, upper = both[:, :TOK], both[:, TOK:]
        back = lax.dot_general(
            g_ref[...], w_out[pl.ds(low, TOK), :], NT, preferred_element_type=F32
        )
        sigma = 1.0 / (1.0 + jnp.exp(-gate))
        active = gate * sigma
        slope = sigma * (1.0 + gate * (1.0 - sigma))
        hidden_ref[:, pl.ds(low, TOK)] = (active * upper).astype(BF16)
        pre_ref[:, pl.ds(low, TOK)] = (back * upper * slope).astype(BF16)
        pre_ref[:, pl.ds(high, TOK)] = (back * active).astype(BF16)

    each_tile(units // TOK, TOK, forward)

    def backward(low):
        rows = lax.dot_general(
            pre_ref[...], w_in[pl.ds(low, HALF), :], NT, preferred_element_type=F32
        ).astype(BF16)
        for j in range(XN):
            backs[j][:, pl.ds(low, HALF)] = rows[j * slot : j * slot + send]

    each_tile(width // HALF, HALF, backward)


def expert(sizes, got, w_in, w_out):
    send, slot = sizes
    units, width = w_out.shape
    rows = XN * slot
    return run(
        functools.partial(expert_kernel, sizes),
        [shaped(send, width)] * XN
        + [shaped(rows, width)] * 2
        + [shaped(rows, units), shaped(rows, 2 * units)],
        [*got, w_in, w_out],
        10 * rows * units * width,
        rows * width * 8,
    )


def combine_kernel(sizes, adds, outs_at, sel_ref, *refs):
    send, slot = sizes
    backs, refs = refs[:XN], refs[XN:]
    incoming, refs = refs[: len(adds)], refs[len(adds) :]
    outs, stacked = refs[:-1], refs[-1]
    width = stacked.shape[1]

    def covers(ref, first, start, stop):
        return first <= start and stop <= first + ref.shape[1]

    def columns(first, low):
        return pl.ds(pl.multiple_of(low - first, TOK), TILE)

    whole = all(r.shape[1] == width for r in (*incoming, *outs))
    spans = [(0, width)] if whole else [(0, width // 2), (width // 2, width)]
    for start, stop in spans:

        def step(offset):
            low = pl.multiple_of(start + offset, TOK)
            here = pl.ds(low, TILE)
            for j, part in enumerate(backs):
                stacked[(j + 1) * slot - 16 : (j + 1) * slot, here] = jnp.zeros(
                    (16, TILE), stacked.dtype
                )
                stacked[j * slot : j * slot + send, here] = part[:, here]
            for out, (block, first) in zip(outs, outs_at):
                if not covers(out, first, start, stop):
                    continue
                total = lax.dot_general(
                    sel_ref[:, block * TOK : (block + 1) * TOK],
                    stacked[:, here],
                    TN,
                    preferred_element_type=F32,
                )
                for ref, (owner, begin) in zip(incoming, adds):
                    if owner == block and covers(ref, begin, start, stop):
                        total = total + ref[:, columns(begin, low)].astype(F32)
                out[:, columns(first, low)] = total.astype(out.dtype)

        each_tile((stop - start) // TILE, TILE, step)


def combine(sizes, sel, backs, incoming, adds, outs_at, outs):
    rows, total = sel.shape
    width = backs[0].shape[1]
    return run(
        functools.partial(combine_kernel, sizes, adds, outs_at),
        outs,
        [sel, *backs, *incoming],
        2 * rows * total * width,
        rows * width * 4,
        scratch=[pltpu.VMEM((rows, width), BF16)],
    )


def weight_kernel(count, turned, *refs):
    out = refs[-1]
    total = sum(
        lax.dot_general(a[...], b[...], TN, preferred_element_type=F32)
        for a, b in zip(refs[:count], refs[count : 2 * count])
    )
    out[...] = (total.T if turned else total).astype(BF16)


def weight_grads(wide, narrow, turned):
    tile = 256
    count = len(wide)
    width, units = wide[0].shape[1], narrow[0].shape[1]
    rows = sum(a.shape[0] for a in wide)
    return pl.pallas_call(
        functools.partial(weight_kernel, count, turned),
        grid=(width // tile,),
        in_specs=[pl.BlockSpec((a.shape[0], tile), lambda i: (0, i)) for a in wide]
        + [pl.BlockSpec(a.shape, lambda i: (0, 0)) for a in narrow],
        out_specs=pl.BlockSpec((units, tile), lambda i: (0, i))
        if turned
        else pl.BlockSpec((tile, units), lambda i: (i, 0)),
        out_shape=shaped(units, width) if turned else shaped(width, units),
        compiler_params=pltpu.CompilerParams(vmem_limit_bytes=VMEM_LIMIT),
        cost_estimate=pl.CostEstimate(
            flops=2 * rows * units * width, bytes_accessed=rows * width * 2, transcendentals=0
        ),
    )(*wide, *narrow)


def along_x(parts):
    moved = [parts[0]]
    for j in range(1, XN):
        pairs = [(x * ZN + z, (x ^ j) * ZN + z) for x in range(XN) for z in range(ZN)]
        moved.append(lax.ppermute(parts[j], "expert", pairs))
    return moved


def along_z(block, side):
    pairs = [
        (x * ZN + z, x * ZN + (((z + side) ^ 1) - side) % ZN)
        for x in range(XN)
        for z in range(ZN)
    ]
    return lax.ppermute(block, "expert", pairs)


def payload(grads, routes, probs):
    first = lax.reduce_precision(probs, 8, 7)
    rest = probs - first
    second = lax.reduce_precision(rest, 8, 7)
    third = rest - second
    table = jnp.concatenate([routes.astype(F32), first, second, third], axis=1).T
    meta = jnp.pad(table, ((0, TOK - table.shape[0]), (0, 0))).astype(BF16)
    return jnp.concatenate([grads, meta], axis=1)


def per_device(saved_inputs, grad_out, routes, route_probs, w_in, w_out):
    sections = lax.axis_size("pipe")
    width = saved_inputs.shape[2]
    half = width // 2
    over = width + TOK
    weight_in, weight_out = w_in[0, 0], w_out[0, 0]
    place = lax.axis_index("expert")
    column, depth = place // ZN, place % ZN
    ids = ((column ^ jnp.arange(XN, dtype=jnp.int32)) * ZN + depth)[None, :]
    sizes = [(round_up(CAP * n, 8), round_up(CAP * n, 16)) for n in (1, 2, 2, 2, 1)]

    own = lax.ppermute(saved_inputs[0], "pipe", [(i, sections - 1 - i) for i in range(sections)])
    pay = payload(grad_out[0], routes[0], route_probs[0])
    a1, b1 = along_z(pay, 0), along_z(pay, 1)
    a2, b2 = along_z(own, 0), along_z(own, 1)
    near_a, near_b = jnp.concatenate([a1, a2], axis=1), jnp.concatenate([b1, b2], axis=1)
    a3, b3 = along_z(near_b, 0), along_z(near_a, 1)
    a4, b4 = along_z(b3, 0), along_z(a3, 1)
    far_grads = along_z(b4[:, :over], 0)
    far_ins = along_z(a4[:, over:], 1)
    blocks = [([(pay, 0)], [(own, 0)])]
    blocks += [
        ([(a, 0), (b, 0)], [(a, over), (b, over)]) for a, b in ((near_a, near_b), (a3, b3), (a4, b4))
    ]
    blocks += [([(far_grads, 0)], [(far_ins, 0)])]
    sels, held, returned = [], [], []
    for n, (grads, ins) in enumerate(blocks):
        rows, sel = pick(sizes[n], width, ids, grads, ins)
        sels.append(sel)
        *backs, x_rows, g_rows, hidden, pre = expert(sizes[n], along_x(rows), weight_in, weight_out)
        held.append((x_rows, g_rows, hidden, pre))
        returned.append(along_x(backs))
    xs, gs, hs, ps = zip(*held)
    grad_w_in = weight_grads(xs, ps, False)
    grad_w_out = weight_grads(gs, hs, True)

    part, full = shaped(TOK, half), shaped(TOK, width)
    side_a, side_b = combine(
        sizes[4], sels[4], returned[4], [], (), ((0, 0), (0, half)), [part, part]
    )
    adds = ((1, 0), (0, half))
    for n in (3, 2, 1):
        incoming = [along_z(side_a, 0), along_z(side_b, 1)]
        side_a, side_b = combine(
            sizes[n], sels[n], returned[n], incoming, adds, ((0, 0), (1, 0)), [full, full]
        )
        adds = ((1, 0), (0, 0))
    incoming = [along_z(side_a, 0), along_z(side_b, 1)]
    (tokens,) = combine(
        sizes[0],
        sels[0],
        returned[0],
        incoming,
        ((0, 0), (0, 0)),
        ((0, 0),),
        [shaped(TOK, width, F32)],
    )
    return tokens[None], grad_w_in[None, None], grad_w_out[None, None]


def solution(mesh):
    rows = P("pipe", "expert", None)
    weights = P("pipe", "expert", None, None)
    return jax.shard_map(
        per_device,
        mesh=mesh,
        in_specs=(rows, rows, rows, rows, weights, weights),
        out_specs=(rows, weights, weights),
        check_vma=False,
    )
```

```python
import functools
import jax
import jax.numpy as jnp
from jax import lax
from jax.experimental import pallas as pl
from jax.experimental.pallas import tpu as pltpu
from jax.sharding import PartitionSpec as P

CAP = 36
XN = 4
ZN = 8
TOK = 128
TILE = 512
F32 = jnp.float32
BF16 = jnp.bfloat16
VMEM_LIMIT = 16 * 1024 * 1024
VMEM = pl.BlockSpec(memory_space=pltpu.VMEM)
NT = (((1,), (1,)), ((), ()))
TN = (((0,), (0,)), ((), ()))


def round_up(value, unit):
    return -(-value // unit) * unit


def shaped(rows, width, kind=BF16):
    return jax.ShapeDtypeStruct((rows, width), kind)


def run(kernel, outs, args, flops, moved, scratch=(), smem=0):
    specs = [pl.BlockSpec(memory_space=pltpu.SMEM)] * smem + [VMEM] * (len(args) - smem)
    return pl.pallas_call(
        kernel,
        out_shape=outs,
        in_specs=specs,
        out_specs=[VMEM] * len(outs),
        scratch_shapes=scratch,
        compiler_params=pltpu.CompilerParams(vmem_limit_bytes=VMEM_LIMIT),
        cost_estimate=pl.CostEstimate(flops=flops, bytes_accessed=moved, transcendentals=0),
    )(*args)


def each_tile(count, size, step):
    def body(i, carry):
        step(pl.multiple_of(i * size, size))
        return carry

    lax.fori_loop(0, count, body, 0)


def select_rows(ids_ref, meta, slot, sel_ref):
    total = meta.shape[1]
    ids = meta[0:8]
    probs = meta[8:16] + meta[16:24] + meta[24:32]
    marks, weights = [], []
    for j in range(XN):
        hit = ids == ids_ref[0, j].astype(F32)
        marks.append(jnp.sum(jnp.where(hit, 1.0, 0.0), axis=0, keepdims=True))
        weights.append(jnp.sum(jnp.where(hit, probs, 0.0), axis=0, keepdims=True))
    mark = jnp.concatenate(marks + [jnp.zeros((8 - XN, total), F32)], axis=0)
    earlier = lax.broadcasted_iota(jnp.int32, (total, total), 0) < lax.broadcasted_iota(
        jnp.int32, (total, total), 1
    )
    rank = jnp.dot(
        mark.astype(BF16), jnp.where(earlier, 1.0, 0.0).astype(BF16), preferred_element_type=F32
    )
    place = lax.broadcasted_iota(jnp.int32, (slot, total), 0).astype(F32)
    scales = []
    for j in range(XN):
        wanted = jnp.where(mark[j : j + 1] > 0.5, rank[j : j + 1], -1.0)
        chosen = place == wanted
        sel_ref[j * slot : (j + 1) * slot, :] = jnp.where(chosen, 1.0, 0.0).astype(BF16)
        scales.append(jnp.sum(jnp.where(chosen, weights[j], 0.0), axis=1, keepdims=True))
    return jnp.concatenate(scales, axis=0)


def pick_kernel(sizes, width, grads, ins, ids_ref, *refs):
    send, slot = sizes
    refs, outs, sel_ref = refs[: -XN - 1], refs[-XN - 1 : -1], refs[-1]
    meta = jnp.concatenate(
        [refs[i][0:32, at + width : at + width + TOK].astype(F32) for i, at in grads], axis=1
    )
    scale = select_rows(ids_ref, meta, slot, sel_ref)
    over = width + TOK
    shared = bool(ins) and all(
        i == k and at + over == to for (i, at), (k, to) in zip(grads, ins)
    )

    def move(blocks, take, put, factor):
        rows = sum(
            jnp.dot(
                sel_ref[:, n * TOK : (n + 1) * TOK],
                refs[i][:, pl.ds(pl.multiple_of(at + take, TOK), TILE)],
                preferred_element_type=F32,
            )
            for n, (i, at) in enumerate(blocks)
        )
        if factor is not None:
            rows = rows * factor
        rows = rows.astype(BF16)
        for j in range(XN):
            outs[j][:, pl.ds(pl.multiple_of(put, TOK), TILE)] = rows[j * slot : j * slot + send]

    if shared:

        def both(low):
            second = (low >= width).astype(jnp.int32)
            factor = jnp.where(low >= width, jnp.ones_like(scale), scale)
            move(grads, low + second * TOK, low, factor)

        each_tile(2 * width // TILE, TILE, both)
    else:
        each_tile(width // TILE, TILE, lambda low: move(grads, low, low, scale))
        if ins:
            each_tile(width // TILE, TILE, lambda low: move(ins, low, width + low, None))


def pick(sizes, width, ids, grads, ins):
    arrays, places = [], []
    for blocks in (grads, ins):
        found = []
        for array, at in blocks:
            index = next((i for i, a in enumerate(arrays) if a is array), None)
            if index is None:
                index = len(arrays)
                arrays.append(array)
            found.append((index, at))
        places.append(tuple(found))
    send, slot = sizes
    total = len(grads) * TOK
    *rows, sel = run(
        functools.partial(pick_kernel, sizes, width, *places),
        [shaped(send, (1 + bool(ins)) * width)] * XN + [shaped(XN * slot, total)],
        [ids, *arrays],
        4 * XN * slot * total * width,
        XN * slot * width * 8,
        smem=1,
    )
    return rows, sel


def pick_in_kernel(sizes, width, places, sel_ref, *refs):
    send, slot = sizes
    refs, outs = refs[:-XN], refs[-XN:]

    def step(low):
        rows = sum(
            jnp.dot(
                sel_ref[:, n * TOK : (n + 1) * TOK],
                refs[n][:, pl.ds(pl.multiple_of(at + low, TOK), TILE)],
                preferred_element_type=F32,
            )
            for n, at in enumerate(places)
        ).astype(BF16)
        for j in range(XN):
            outs[j][:, pl.ds(low, TILE)] = rows[j * slot : j * slot + send]

    each_tile(width // TILE, TILE, step)


def pick_ins(sizes, width, sel, ins):
    send, slot = sizes
    return run(
        functools.partial(pick_in_kernel, sizes, width, tuple(at for _, at in ins)),
        [shaped(send, width)] * XN,
        [sel, *(array for array, _ in ins)],
        2 * XN * slot * len(ins) * TOK * width,
        XN * slot * width * 4,
    )


def stack_rows(dst, parts, sizes, base):
    send, slot = sizes

    def step(low):
        for j, part in enumerate(parts):
            dst[(j + 1) * slot - 16 : (j + 1) * slot, pl.ds(low, TILE)] = jnp.zeros(
                (16, TILE), dst.dtype
            )
            dst[j * slot : j * slot + send, pl.ds(low, TILE)] = part[
                :, pl.ds(pl.multiple_of(base + low, TOK), TILE)
            ]

    each_tile(dst.shape[1] // TILE, TILE, step)


def expert_kernel(sizes, *refs):
    send, slot = sizes
    rows, (w_in, w_out) = refs[:XN], refs[XN : XN + 2]
    backs, (x_ref, g_ref, hidden_ref, pre_ref) = refs[XN + 2 : 2 * XN + 2], refs[2 * XN + 2 :]
    units, width = w_out.shape
    stack_rows(x_ref, rows, sizes, width)
    stack_rows(g_ref, rows, sizes, 0)

    def forward(low):
        high = pl.multiple_of(units + low, TOK)
        pair = jnp.concatenate([w_in[:, pl.ds(low, TOK)], w_in[:, pl.ds(high, TOK)]], axis=1)
        both = jnp.dot(x_ref[...], pair, preferred_element_type=F32)
        gate, upper = both[:, :TOK], both[:, TOK:]
        back = lax.dot_general(
            g_ref[...], w_out[pl.ds(low, TOK), :], NT, preferred_element_type=F32
        )
        sigma = 1.0 / (1.0 + jnp.exp(-gate))
        active = gate * sigma
        slope = sigma * (1.0 + gate * (1.0 - sigma))
        hidden_ref[:, pl.ds(low, TOK)] = (active * upper).astype(BF16)
        pre_ref[:, pl.ds(low, TOK)] = (back * upper * slope).astype(BF16)
        pre_ref[:, pl.ds(high, TOK)] = (back * active).astype(BF16)

    each_tile(units // TOK, TOK, forward)

    def backward(low):
        rows = lax.dot_general(
            pre_ref[...], w_in[pl.ds(low, TILE), :], NT, preferred_element_type=F32
        ).astype(BF16)
        for j in range(XN):
            backs[j][:, pl.ds(low, TILE)] = rows[j * slot : j * slot + send]

    each_tile(width // TILE, TILE, backward)


def expert(sizes, got, w_in, w_out):
    send, slot = sizes
    units, width = w_out.shape
    rows = XN * slot
    return run(
        functools.partial(expert_kernel, sizes),
        [shaped(send, width)] * XN
        + [shaped(rows, width)] * 2
        + [shaped(rows, units), shaped(rows, 2 * units)],
        [*got, w_in, w_out],
        10 * rows * units * width,
        rows * width * 8,
    )


def combine_kernel(sizes, adds, outs_at, sel_ref, *refs):
    send, slot = sizes
    backs, refs = refs[:XN], refs[XN:]
    incoming, refs = refs[: len(adds)], refs[len(adds) :]
    outs, stacked = refs[:-1], refs[-1]
    width = stacked.shape[1]

    def covers(ref, first, start, stop):
        return first <= start and stop <= first + ref.shape[1]

    def columns(first, low):
        return pl.ds(pl.multiple_of(low - first, TOK), TILE)

    whole = all(r.shape[1] == width for r in (*incoming, *outs))
    spans = [(0, width)] if whole else [(0, width // 2), (width // 2, width)]
    for start, stop in spans:

        def step(offset):
            low = pl.multiple_of(start + offset, TOK)
            here = pl.ds(low, TILE)
            for j, part in enumerate(backs):
                stacked[(j + 1) * slot - 16 : (j + 1) * slot, here] = jnp.zeros(
                    (16, TILE), stacked.dtype
                )
                stacked[j * slot : j * slot + send, here] = part[0:send, here]
            for out, (block, first) in zip(outs, outs_at):
                if not covers(out, first, start, stop):
                    continue
                total = lax.dot_general(
                    sel_ref[:, block * TOK : (block + 1) * TOK],
                    stacked[:, here],
                    TN,
                    preferred_element_type=F32,
                )
                for ref, (owner, begin) in zip(incoming, adds):
                    if owner == block and covers(ref, begin, start, stop):
                        total = total + ref[:, columns(begin, low)].astype(F32)
                out[:, columns(first, low)] = total.astype(out.dtype)

        each_tile((stop - start) // TILE, TILE, step)


def combine(sizes, sel, backs, incoming, adds, outs_at, outs):
    rows, total = sel.shape
    width = backs[0].shape[1]
    return run(
        functools.partial(combine_kernel, sizes, adds, outs_at),
        outs,
        [sel, *backs, *incoming],
        2 * rows * total * width,
        rows * width * 4,
        scratch=[pltpu.VMEM((rows, width), BF16)],
    )


def weight_kernel(count, turned, *refs):
    out = refs[-1]
    total = sum(
        lax.dot_general(a[...], b[...], TN, preferred_element_type=F32)
        for a, b in zip(refs[:count], refs[count : 2 * count])
    )
    out[...] = (total.T if turned else total).astype(BF16)


def weight_grads(wide, narrow, turned):
    tile = 256
    count = len(wide)
    width, units = wide[0].shape[1], narrow[0].shape[1]
    rows = sum(a.shape[0] for a in wide)
    return pl.pallas_call(
        functools.partial(weight_kernel, count, turned),
        grid=(width // tile,),
        in_specs=[pl.BlockSpec((a.shape[0], tile), lambda i: (0, i)) for a in wide]
        + [pl.BlockSpec(a.shape, lambda i: (0, 0)) for a in narrow],
        out_specs=pl.BlockSpec((units, tile), lambda i: (0, i))
        if turned
        else pl.BlockSpec((tile, units), lambda i: (i, 0)),
        out_shape=shaped(units, width) if turned else shaped(width, units),
        compiler_params=pltpu.CompilerParams(vmem_limit_bytes=VMEM_LIMIT),
        cost_estimate=pl.CostEstimate(
            flops=2 * rows * units * width, bytes_accessed=rows * width * 2, transcendentals=0
        ),
    )(*wide, *narrow)


def along_x(parts):
    moved = [parts[0]]
    for j in range(1, XN):
        pairs = [(x * ZN + z, (x ^ j) * ZN + z) for x in range(XN) for z in range(ZN)]
        moved.append(lax.ppermute(parts[j], "expert", pairs))
    return moved


def along_z(block, side):
    pairs = [
        (x * ZN + z, x * ZN + (((z + side) ^ 1) - side) % ZN)
        for x in range(XN)
        for z in range(ZN)
    ]
    return lax.ppermute(block, "expert", pairs)


def payload(grads, routes, probs):
    first = lax.reduce_precision(probs, 8, 7)
    rest = probs - first
    second = lax.reduce_precision(rest, 8, 7)
    third = rest - second
    table = jnp.concatenate([routes.astype(F32), first, second, third], axis=1).T
    meta = jnp.pad(table, ((0, TOK - table.shape[0]), (0, 0))).astype(BF16)
    return jnp.concatenate([grads, meta], axis=1)


def per_device(saved_inputs, grad_out, routes, route_probs, w_in, w_out):
    sections = lax.axis_size("pipe")
    width = saved_inputs.shape[2]
    half = width // 2
    over = width + TOK
    weight_in, weight_out = w_in[0, 0], w_out[0, 0]
    place = lax.axis_index("expert")
    column, depth = place // ZN, place % ZN
    ids = ((column ^ jnp.arange(XN, dtype=jnp.int32)) * ZN + depth)[None, :]
    sizes = [(round_up(CAP * n, 8), round_up(CAP * n, 16)) for n in (1, 2, 2, 2, 1)]

    own = lax.ppermute(saved_inputs[0], "pipe", [(i, sections - 1 - i) for i in range(sections)])
    pay = payload(grad_out[0], routes[0], route_probs[0])
    a1, b1 = along_z(pay, 0), along_z(pay, 1)
    a2, b2 = along_z(own, 0), along_z(own, 1)
    near_a, near_b = jnp.concatenate([a1, a2], axis=1), jnp.concatenate([b1, b2], axis=1)
    a3, b3 = along_z(near_b, 0), along_z(near_a, 1)
    a4, b4 = along_z(b3, 0), along_z(a3, 1)
    far_grads = along_z(b4[:, :over], 0)
    far_ins = along_z(a4[:, over:], 1)
    blocks = [([(pay, 0)], [(own, 0)])]
    blocks += [
        ([(a, 0), (b, 0)], [(a, over), (b, over)]) for a, b in ((near_a, near_b), (a3, b3), (a4, b4))
    ]
    blocks += [([(far_grads, 0)], [(far_ins, 0)])]
    sels, held, kept = [], [], []
    for n, (grads, ins) in enumerate(blocks):
        if n == 3:
            rows, sel = pick(sizes[n], width, ids, grads, ())
            got_grads = along_x(rows)
            got_ins = along_x(pick_ins(sizes[n], width, sel, ins))
            got = [jnp.concatenate([got_grads[0], got_ins[0]], axis=1)]
            got += [
                jnp.concatenate(pair, axis=1) for pair in zip(got_grads[1:], got_ins[1:])
            ]
        else:
            rows, sel = pick(sizes[n], width, ids, grads, ins)
            got = along_x(rows)
        sels.append(sel)
        *backs, x_rows, g_rows, hidden, pre = expert(sizes[n], got, weight_in, weight_out)
        held.append((x_rows, g_rows, hidden, pre))
        kept.append(backs)
    cut = sizes[1][0]
    both = along_x([jnp.concatenate(pair, axis=0) for pair in zip(kept[1], kept[0])])
    tails = [part[cut:] for part in both[1:]]
    returned = [[kept[0][0], *tails], [kept[1][0], *both[1:]]]
    returned += [along_x(kept[n]) for n in (2, 3, 4)]
    xs, gs, hs, ps = zip(*held)
    grad_w_in = weight_grads(xs, ps, False)
    grad_w_out = weight_grads(gs, hs, True)

    part, full = shaped(TOK, half), shaped(TOK, width)
    side_a, side_b = combine(
        sizes[4], sels[4], returned[4], [], (), ((0, 0), (0, half)), [part, part]
    )
    adds = ((1, 0), (0, half))
    for n in (3, 2, 1):
        incoming = [along_z(side_a, 0), along_z(side_b, 1)]
        side_a, side_b = combine(
            sizes[n], sels[n], returned[n], incoming, adds, ((0, 0), (1, 0)), [full, full]
        )
        adds = ((1, 0), (0, 0))
    incoming = [along_z(side_a, 0), along_z(side_b, 1)]
    (tokens,) = combine(
        sizes[0],
        sels[0],
        returned[0],
        incoming,
        ((0, 0), (0, 0)),
        ((0, 0),),
        [shaped(TOK, width, F32)],
    )
    return tokens[None], grad_w_in[None, None], grad_w_out[None, None]


def solution(mesh):
    rows = P("pipe", "expert", None)
    weights = P("pipe", "expert", None, None)
    return jax.shard_map(
        per_device,
        mesh=mesh,
        in_specs=(rows, rows, rows, rows, weights, weights),
        out_specs=(rows, weights, weights),
        check_vma=False,
    )
```

```python
import functools
import jax
import jax.numpy as jnp
from jax import lax
from jax.experimental import pallas as pl
from jax.experimental.pallas import tpu as pltpu
from jax.sharding import PartitionSpec as P

CAP = 36
XN = 4
ZN = 8
TOK = 128
TILE = 512
WIDE = 1024
F32 = jnp.float32
BF16 = jnp.bfloat16
VMEM_LIMIT = 16 * 1024 * 1024
VMEM = pl.BlockSpec(memory_space=pltpu.VMEM)
NT = (((1,), (1,)), ((), ()))
TN = (((0,), (0,)), ((), ()))


def round_up(value, unit):
    return -(-value // unit) * unit


def shaped(rows, width, kind=BF16):
    return jax.ShapeDtypeStruct((rows, width), kind)


def run(kernel, outs, args, flops, moved, scratch=(), smem=0):
    specs = [pl.BlockSpec(memory_space=pltpu.SMEM)] * smem + [VMEM] * (len(args) - smem)
    return pl.pallas_call(
        kernel,
        out_shape=outs,
        in_specs=specs,
        out_specs=[VMEM] * len(outs),
        scratch_shapes=scratch,
        compiler_params=pltpu.CompilerParams(vmem_limit_bytes=VMEM_LIMIT),
        cost_estimate=pl.CostEstimate(flops=flops, bytes_accessed=moved, transcendentals=0),
    )(*args)


def each_tile(count, size, step):
    def body(i, carry):
        step(pl.multiple_of(i * size, size))
        return carry

    lax.fori_loop(0, count, body, 0)


def select_rows(ids_ref, meta, slot, sel_ref):
    total = meta.shape[1]
    ids = meta[0:8]
    probs = meta[8:16] + meta[16:24] + meta[24:32]
    marks, weights = [], []
    for j in range(XN):
        hit = ids == ids_ref[0, j].astype(F32)
        marks.append(jnp.sum(jnp.where(hit, 1.0, 0.0), axis=0, keepdims=True))
        weights.append(jnp.sum(jnp.where(hit, probs, 0.0), axis=0, keepdims=True))
    mark = jnp.concatenate(marks + [jnp.zeros((8 - XN, total), F32)], axis=0)
    earlier = lax.broadcasted_iota(jnp.int32, (total, total), 0) < lax.broadcasted_iota(
        jnp.int32, (total, total), 1
    )
    rank = jnp.dot(
        mark.astype(BF16), jnp.where(earlier, 1.0, 0.0).astype(BF16), preferred_element_type=F32
    )
    place = lax.broadcasted_iota(jnp.int32, (slot, total), 0).astype(F32)
    scales = []
    for j in range(XN):
        wanted = jnp.where(mark[j : j + 1] > 0.5, rank[j : j + 1], -1.0)
        chosen = place == wanted
        sel_ref[j * slot : (j + 1) * slot, :] = jnp.where(chosen, 1.0, 0.0).astype(BF16)
        scales.append(jnp.sum(jnp.where(chosen, weights[j], 0.0), axis=1, keepdims=True))
    return jnp.concatenate(scales, axis=0)


def pick_kernel(sizes, width, grads, ins, ids_ref, *refs):
    send, slot = sizes
    refs, outs, sel_ref = refs[: -XN - 1], refs[-XN - 1 : -1], refs[-1]
    meta = jnp.concatenate(
        [refs[i][0:32, at + width : at + width + TOK].astype(F32) for i, at in grads], axis=1
    )
    scale = select_rows(ids_ref, meta, slot, sel_ref)
    over = width + TOK
    shared = bool(ins) and all(
        i == k and at + over == to for (i, at), (k, to) in zip(grads, ins)
    )

    def move(blocks, take, put, factor):
        rows = sum(
            jnp.dot(
                sel_ref[:, n * TOK : (n + 1) * TOK],
                refs[i][:, pl.ds(pl.multiple_of(at + take, TOK), TILE)],
                preferred_element_type=F32,
            )
            for n, (i, at) in enumerate(blocks)
        )
        if factor is not None:
            rows = rows * factor
        rows = rows.astype(BF16)
        for j in range(XN):
            outs[j][:, pl.ds(pl.multiple_of(put, TOK), TILE)] = rows[j * slot : j * slot + send]

    if shared:

        def both(low):
            second = (low >= width).astype(jnp.int32)
            factor = jnp.where(low >= width, jnp.ones_like(scale), scale)
            move(grads, low + second * TOK, low, factor)

        each_tile(2 * width // TILE, TILE, both)
    else:
        each_tile(width // TILE, TILE, lambda low: move(grads, low, low, scale))
        if ins:
            each_tile(width // TILE, TILE, lambda low: move(ins, low, width + low, None))


def pick(sizes, width, ids, grads, ins):
    arrays, places = [], []
    for blocks in (grads, ins):
        found = []
        for array, at in blocks:
            index = next((i for i, a in enumerate(arrays) if a is array), None)
            if index is None:
                index = len(arrays)
                arrays.append(array)
            found.append((index, at))
        places.append(tuple(found))
    send, slot = sizes
    total = len(grads) * TOK
    *rows, sel = run(
        functools.partial(pick_kernel, sizes, width, *places),
        [shaped(send, (1 + bool(ins)) * width)] * XN + [shaped(XN * slot, total)],
        [ids, *arrays],
        4 * XN * slot * total * width,
        XN * slot * width * 8,
        smem=1,
    )
    return rows, sel


def pick_in_kernel(sizes, width, places, sel_ref, *refs):
    send, slot = sizes
    refs, outs = refs[:-XN], refs[-XN:]

    def step(low):
        rows = sum(
            jnp.dot(
                sel_ref[:, n * TOK : (n + 1) * TOK],
                refs[n][:, pl.ds(pl.multiple_of(at + low, TOK), TILE)],
                preferred_element_type=F32,
            )
            for n, at in enumerate(places)
        ).astype(BF16)
        for j in range(XN):
            outs[j][:, pl.ds(low, TILE)] = rows[j * slot : j * slot + send]

    each_tile(width // TILE, TILE, step)


def pick_ins(sizes, width, sel, ins):
    send, slot = sizes
    return run(
        functools.partial(pick_in_kernel, sizes, width, tuple(at for _, at in ins)),
        [shaped(send, width)] * XN,
        [sel, *(array for array, _ in ins)],
        2 * XN * slot * len(ins) * TOK * width,
        XN * slot * width * 4,
    )


def stack_rows(dst, parts, sizes, base):
    send, slot = sizes

    def step(low):
        for j, part in enumerate(parts):
            dst[(j + 1) * slot - 16 : (j + 1) * slot, pl.ds(low, TILE)] = jnp.zeros(
                (16, TILE), dst.dtype
            )
            dst[j * slot : j * slot + send, pl.ds(low, TILE)] = part[
                :, pl.ds(pl.multiple_of(base + low, TOK), TILE)
            ]

    each_tile(dst.shape[1] // TILE, TILE, step)


def expert_kernel(sizes, *refs):
    send, slot = sizes
    rows, (w_in, w_out) = refs[:XN], refs[XN : XN + 2]
    backs, (x_ref, g_ref, hidden_ref, pre_ref) = refs[XN + 2 : 2 * XN + 2], refs[2 * XN + 2 :]
    units, width = w_out.shape
    stack_rows(x_ref, rows, sizes, width)
    stack_rows(g_ref, rows, sizes, 0)

    def forward(low):
        high = pl.multiple_of(units + low, TOK)
        pair = jnp.concatenate([w_in[:, pl.ds(low, TOK)], w_in[:, pl.ds(high, TOK)]], axis=1)
        both = jnp.dot(x_ref[...], pair, preferred_element_type=F32)
        gate, upper = both[:, :TOK], both[:, TOK:]
        back = lax.dot_general(
            g_ref[...], w_out[pl.ds(low, TOK), :], NT, preferred_element_type=F32
        )
        sigma = 1.0 / (1.0 + jnp.exp(-gate))
        active = gate * sigma
        slope = sigma * (1.0 + gate * (1.0 - sigma))
        hidden_ref[:, pl.ds(low, TOK)] = (active * upper).astype(BF16)
        pre_ref[:, pl.ds(low, TOK)] = (back * upper * slope).astype(BF16)
        pre_ref[:, pl.ds(high, TOK)] = (back * active).astype(BF16)

    each_tile(units // TOK, TOK, forward)

    def backward(low):
        rows = lax.dot_general(
            pre_ref[...], w_in[pl.ds(low, TILE), :], NT, preferred_element_type=F32
        ).astype(BF16)
        for j in range(XN):
            backs[j][:, pl.ds(low, TILE)] = rows[j * slot : j * slot + send]

    each_tile(width // TILE, TILE, backward)


def expert(sizes, got, w_in, w_out):
    send, slot = sizes
    units, width = w_out.shape
    rows = XN * slot
    return run(
        functools.partial(expert_kernel, sizes),
        [shaped(send, width)] * XN
        + [shaped(rows, width)] * 2
        + [shaped(rows, units), shaped(rows, 2 * units)],
        [*got, w_in, w_out],
        10 * rows * units * width,
        rows * width * 8,
    )


def combine_kernel(sizes, adds, outs_at, sel_ref, *refs):
    send, slot = sizes
    backs, refs = refs[:XN], refs[XN:]
    incoming, refs = refs[: len(adds)], refs[len(adds) :]
    outs, stacked = refs[:-1], refs[-1]
    width = stacked.shape[1]

    def covers(ref, first, start, stop):
        return first <= start and stop <= first + ref.shape[1]

    def columns(first, low):
        return pl.ds(pl.multiple_of(low - first, TOK), tile)

    whole = all(r.shape[1] == width for r in (*incoming, *outs))
    tile = WIDE if whole and len(outs) == 2 else TILE
    spans = [(0, width)] if whole else [(0, width // 2), (width // 2, width)]
    for start, stop in spans:

        def step(offset):
            low = pl.multiple_of(start + offset, TOK)
            here = pl.ds(low, tile)
            for j, part in enumerate(backs):
                stacked[(j + 1) * slot - 16 : (j + 1) * slot, here] = jnp.zeros(
                    (16, tile), stacked.dtype
                )
                stacked[j * slot : j * slot + send, here] = part[0:send, here]
            for out, (block, first) in zip(outs, outs_at):
                if not covers(out, first, start, stop):
                    continue
                total = lax.dot_general(
                    sel_ref[:, block * TOK : (block + 1) * TOK],
                    stacked[:, here],
                    TN,
                    preferred_element_type=F32,
                )
                for ref, (owner, begin) in zip(incoming, adds):
                    if owner == block and covers(ref, begin, start, stop):
                        total = total + ref[:, columns(begin, low)].astype(F32)
                out[:, columns(first, low)] = total.astype(out.dtype)

        each_tile((stop - start) // tile, tile, step)


def combine(sizes, sel, backs, incoming, adds, outs_at, outs):
    rows, total = sel.shape
    width = backs[0].shape[1]
    return run(
        functools.partial(combine_kernel, sizes, adds, outs_at),
        outs,
        [sel, *backs, *incoming],
        2 * rows * total * width,
        rows * width * 4,
        scratch=[pltpu.VMEM((rows, width), BF16)],
    )


def weight_kernel(count, turned, *refs):
    out = refs[-1]
    total = sum(
        lax.dot_general(a[...], b[...], TN, preferred_element_type=F32)
        for a, b in zip(refs[:count], refs[count : 2 * count])
    )
    out[...] = (total.T if turned else total).astype(BF16)


def weight_grads(wide, narrow, turned):
    tile = 256
    count = len(wide)
    width, units = wide[0].shape[1], narrow[0].shape[1]
    rows = sum(a.shape[0] for a in wide)
    return pl.pallas_call(
        functools.partial(weight_kernel, count, turned),
        grid=(width // tile,),
        in_specs=[pl.BlockSpec((a.shape[0], tile), lambda i: (0, i)) for a in wide]
        + [pl.BlockSpec(a.shape, lambda i: (0, 0)) for a in narrow],
        out_specs=pl.BlockSpec((units, tile), lambda i: (0, i))
        if turned
        else pl.BlockSpec((tile, units), lambda i: (i, 0)),
        out_shape=shaped(units, width) if turned else shaped(width, units),
        compiler_params=pltpu.CompilerParams(vmem_limit_bytes=VMEM_LIMIT),
        cost_estimate=pl.CostEstimate(
            flops=2 * rows * units * width, bytes_accessed=rows * width * 2, transcendentals=0
        ),
    )(*wide, *narrow)


def along_x(parts):
    moved = [parts[0]]
    for j in range(1, XN):
        pairs = [(x * ZN + z, (x ^ j) * ZN + z) for x in range(XN) for z in range(ZN)]
        moved.append(lax.ppermute(parts[j], "expert", pairs))
    return moved


def along_z(block, side):
    pairs = [
        (x * ZN + z, x * ZN + (((z + side) ^ 1) - side) % ZN)
        for x in range(XN)
        for z in range(ZN)
    ]
    return lax.ppermute(block, "expert", pairs)


def payload(grads, routes, probs):
    first = lax.reduce_precision(probs, 8, 7)
    rest = probs - first
    second = lax.reduce_precision(rest, 8, 7)
    third = rest - second
    table = jnp.concatenate([routes.astype(F32), first, second, third], axis=1).T
    meta = jnp.pad(table, ((0, TOK - table.shape[0]), (0, 0))).astype(BF16)
    return jnp.concatenate([grads, meta], axis=1)


def per_device(saved_inputs, grad_out, routes, route_probs, w_in, w_out):
    sections = lax.axis_size("pipe")
    width = saved_inputs.shape[2]
    half = width // 2
    over = width + TOK
    weight_in, weight_out = w_in[0, 0], w_out[0, 0]
    place = lax.axis_index("expert")
    column, depth = place // ZN, place % ZN
    ids = ((column ^ jnp.arange(XN, dtype=jnp.int32)) * ZN + depth)[None, :]
    sizes = [(round_up(CAP * n, 8), round_up(CAP * n, 16)) for n in (1, 2, 2, 2, 1)]

    own = lax.ppermute(saved_inputs[0], "pipe", [(i, sections - 1 - i) for i in range(sections)])
    pay = payload(grad_out[0], routes[0], route_probs[0])
    a1, b1 = along_z(pay, 0), along_z(pay, 1)
    a2, b2 = along_z(own, 0), along_z(own, 1)
    near_a, near_b = jnp.concatenate([a1, a2], axis=1), jnp.concatenate([b1, b2], axis=1)
    a3, b3 = along_z(near_b, 0), along_z(near_a, 1)
    a4, b4 = along_z(b3, 0), along_z(a3, 1)
    far_grads = along_z(b4[:, :over], 0)
    far_ins = along_z(a4[:, over:], 1)
    blocks = [([(pay, 0)], [(own, 0)])]
    blocks += [
        ([(a, 0), (b, 0)], [(a, over), (b, over)]) for a, b in ((near_a, near_b), (a3, b3), (a4, b4))
    ]
    blocks += [([(far_grads, 0)], [(far_ins, 0)])]
    sels, held, kept = [], [], []
    for n, (grads, ins) in enumerate(blocks):
        if n == 3:
            rows, sel = pick(sizes[n], width, ids, grads, ())
            got_grads = along_x(rows)
            got_ins = along_x(pick_ins(sizes[n], width, sel, ins))
            got = [jnp.concatenate([got_grads[0], got_ins[0]], axis=1)]
            got += [
                jnp.concatenate(pair, axis=1) for pair in zip(got_grads[1:], got_ins[1:])
            ]
        else:
            rows, sel = pick(sizes[n], width, ids, grads, ins)
            got = along_x(rows)
        sels.append(sel)
        *backs, x_rows, g_rows, hidden, pre = expert(sizes[n], got, weight_in, weight_out)
        held.append((x_rows, g_rows, hidden, pre))
        kept.append(backs)
    cut = sizes[1][0]
    both = along_x([jnp.concatenate(pair, axis=0) for pair in zip(kept[1], kept[0])])
    tails = [part[cut:] for part in both[1:]]
    returned = [[kept[0][0], *tails], [kept[1][0], *both[1:]]]
    returned += [along_x(kept[n]) for n in (2, 3, 4)]
    xs, gs, hs, ps = zip(*held)
    grad_w_in = weight_grads(xs, ps, False)
    grad_w_out = weight_grads(gs, hs, True)

    part, full = shaped(TOK, half), shaped(TOK, width)
    side_a, side_b = combine(
        sizes[4], sels[4], returned[4], [], (), ((0, 0), (0, half)), [part, part]
    )
    adds = ((1, 0), (0, half))
    for n in (3, 2, 1):
        incoming = [along_z(side_a, 0), along_z(side_b, 1)]
        side_a, side_b = combine(
            sizes[n], sels[n], returned[n], incoming, adds, ((0, 0), (1, 0)), [full, full]
        )
        adds = ((1, 0), (0, 0))
    incoming = [along_z(side_a, 0), along_z(side_b, 1)]
    (tokens,) = combine(
        sizes[0],
        sels[0],
        returned[0],
        incoming,
        ((0, 0), (0, 0)),
        ((0, 0),),
        [shaped(TOK, width, F32)],
    )
    return tokens[None], grad_w_in[None, None], grad_w_out[None, None]


def solution(mesh):
    rows = P("pipe", "expert", None)
    weights = P("pipe", "expert", None, None)
    return jax.shard_map(
        per_device,
        mesh=mesh,
        in_specs=(rows, rows, rows, rows, weights, weights),
        out_specs=(rows, weights, weights),
        check_vma=False,
    )
```
